256 devices in a mesh: chan: 8 (over x, y_lo), win: 32 (over y_hi, z, core).
Axes of the slice: x: 4, y: 4 (y_hi: 2, y_lo: 2; y = y_hi * 2 + y_lo), z: 8, core: 2. Of those that a mesh axis runs over, the one named last changes fastest.
Arguments:
- spectra: bfloat16 [768, 32, 2, 4096], P('win', None, None, 'chan'), may hold values from -500 to 500, as said below
- flags: int32 [768], P('win'), may hold values 0 or 1
- pair_table: int32 [8, 8], replicated, may hold values from 0 to 7, each once within a row
Outputs:
- stacks: bfloat16 [32, 2, 4096, 4096], P('win', None, 'chan')
The draws below stay inside these ranges and needn't reach their ends.
Inputs may be any that keep to these rules, and one draw needn't show every extreme that they name: `spectra`: spectra whose amplitudes vary from window to window, channel to channel and bin to bin. `pair_table`: each row is an ordering of the 8 channel blocks.
All inputs are finite; a program needn't handle non-finite values. No bound on the sum of `flags` on one device may be relied on, other than what follows from the above.
Results may differ from the reference program's by a relative error of at most 0.0067.
Values may be sent and summed in bfloat16 or wider, within the bound.
A program may use at most 64 MiB of HBM per device.

```python
import math
import jax
import jax.numpy as jnp
from jax import lax

NCH = 4096
F = 32
WINDOWS = 768
NB = 8
CB = 512


def draw_spectra(key, part):
    keys = jax.random.split(key, 3)
    shape = (WINDOWS, F, 2, NCH)
    row_scale = jnp.exp(jax.random.uniform(keys[0], (WINDOWS, 1, 1, NCH), jnp.float32, 0.0, math.log(10.0)))
    bin_scale = jnp.exp(jax.random.uniform(keys[1], (1, F, 1, NCH), jnp.float32, 0.0, math.log(10.0)))
    base = jnp.clip(jax.random.normal(keys[2], shape, jnp.float32), -5.0, 5.0)
    values = base * row_scale * bin_scale
    return values.astype(jnp.bfloat16)


def set_ends(array, stream_key, least, largest):
    longest = array.shape.index(max(array.shape))
    spots = []
    for shift in (0, 1):
        where = [jax.random.randint(jax.random.fold_in(stream_key, axis), (), 0, length) for axis, length in enumerate(array.shape)]
        where[longest] = (where[longest] + shift) % array.shape[longest]
        spots.append(tuple(where))
    return array.at[spots[0]].set(least).at[spots[1]].set(largest)


def setup_inputs(seed: int = 0) -> dict:
    seeds = jax.random.split(jax.random.key(seed), 4)
    spectra = draw_spectra(jax.random.fold_in(seeds[3], 71), 0)
    flags = set_ends((jax.random.randint(seeds[1], (WINDOWS,), 0, 4) < 3).astype(jnp.int32), jax.random.fold_in(seeds[1], 1), 0, 1)
    pair_table = jax.vmap(lambda own: jax.random.permutation(own, NB))(jax.random.split(seeds[2], NB)).reshape((NB, NB)).astype(jnp.int32)
    return {"spectra": spectra, "flags": flags, "pair_table": pair_table}


EPSILON = 1e-05

def reference(spectra, flags, pair_table):
    raw_values = spectra.astype(jnp.float32)
    band_power = lax.optimization_barrier(jnp.mean(raw_values * raw_values, axis=(1, 2), keepdims=True))
    validity = flags.astype(jnp.float32)[:, None, None, None]
    tempered = (raw_values * lax.rsqrt(band_power + EPSILON) * validity).astype(jnp.bfloat16)
    tempered_wide = tempered.astype(jnp.float32)
    bin_power = lax.optimization_barrier(jnp.mean(tempered_wide * tempered_wide, axis=(0, 2), keepdims=True))
    whitened = (tempered_wide * lax.rsqrt(bin_power + EPSILON)).astype(jnp.bfloat16)
    stack_scale = 1.0 / math.sqrt(WINDOWS)

    def one_bin(index):
        block = lax.dynamic_index_in_dim(whitened, index, 1, keepdims=False)
        real_part = block[:, 0, :]
        imag_part = block[:, 1, :]
        cross_re = jnp.dot(real_part.T, real_part, preferred_element_type=jnp.float32) + jnp.dot(imag_part.T, imag_part, preferred_element_type=jnp.float32)
        cross_im = jnp.dot(imag_part.T, real_part, preferred_element_type=jnp.float32) - jnp.dot(real_part.T, imag_part, preferred_element_type=jnp.float32)
        whole = jnp.stack([cross_re, cross_im]) * stack_scale
        blocked = whole.reshape(2, NB, CB, NB, CB)
        ordered = jax.vmap(lambda rows, order: rows[:, :, order, :], in_axes=(1, 0), out_axes=1)(blocked, pair_table)
        return ordered.reshape(2, NCH, NCH).astype(jnp.bfloat16)
    return lax.map(one_bin, jnp.arange(F, dtype=jnp.int32))
```

```python
import functools
import math

import jax
import jax.numpy as jnp
from jax import lax
from jax.experimental import pallas as pl
from jax.experimental.pallas import tpu as pltpu
from jax.sharding import PartitionSpec as P

EPSILON = 1e-05
MESH = pl.DeviceIdType.MESH

NX = 4
NZ = 8
GROUPS = 8
OFFSETS = (0, 1, -1, 2, -2, 3, -3, 4)
NBLK = 8
HALF = 96
CUT_LO = 64
CUT_HI = 144


def gather_stack_kernel(
    chunk_rows,
    tempered,
    prod,
    x_all,
    acc,
    left,
    colpow,
    rowpow,
    a2a_send,
    a2a_recv,
    local_sem,
    ag_send,
    recv1,
    recv2,
    recv3,
    *,
    windows,
):
    c = lax.axis_index("chan")
    w = lax.axis_index("win")
    x, yl = c // 2, c % 2
    yh, z, core = w // 16, (w // 2) % NZ, w % 2
    xp = (x + 1 + 2 * core) % NX
    xm = (x + 3 + 2 * core) % NX
    x2 = (x + 2) % NX

    def src(xx, yy):
        return 2 * xx + yy

    own = src(x, yl)
    pair = src(x, 1 - yl)
    dev_p = (src(xp, yl), w)
    dev_m = (src(xm, yl), w)
    dev_y = (pair, w)

    def peer(zz, other_half, other_core):
        cc = c if not other_half else pair
        hh = yh if not other_half else 1 - yh
        kk = core if not other_core else 1 - core
        return (cc, hh * 16 + zz * 2 + kk)

    barrier = pltpu.get_barrier_semaphore()
    count = 0
    for off in OFFSETS:
        zz = (z - off) % NZ
        for other_half in (0, 1):
            for other_core in (0, 1):
                if off == 0 and not other_half and not other_core:
                    continue
                pl.semaphore_signal(
                    barrier, inc=1, device_id=peer(zz, other_half, other_core), device_id_type=MESH
                )
                count += 1
    for dev in (dev_p, dev_m, dev_y):
        pl.semaphore_signal(barrier, inc=1, device_id=dev, device_id_type=MESH)
        count += 1
    pl.semaphore_wait(barrier, count)

    local = None
    for g, off in enumerate(OFFSETS):
        zz = (z - off) % NZ
        for other_half in (0, 1):
            for other_core in (0, 1):
                dev = peer(zz, other_half, other_core)
                row = other_half * HALF + core * chunk_rows
                row = pl.multiple_of(row, 16)
                if off == 0 and not other_half and not other_core:
                    local = pltpu.make_async_copy(
                        tempered.at[w], x_all.at[own, g, pl.ds(row, chunk_rows)], local_sem
                    )
                    local.start()
                    continue
                entry = own if not other_half else pair
                pltpu.make_async_remote_copy(
                    src_ref=tempered.at[dev[1]],
                    dst_ref=x_all.at[entry, g, pl.ds(row, chunk_rows)],
                    send_sem=a2a_send,
                    recv_sem=a2a_recv.at[g],
                    device_id=dev,
                    device_id_type=MESH,
                ).start()

    def send(s, g, lo, hi, recv_sem, dev):
        ref = x_all.at[s, g, pl.ds(lo, hi - lo)]
        pltpu.make_async_remote_copy(
            src_ref=ref,
            dst_ref=ref,
            send_sem=ag_send,
            recv_sem=recv_sem,
            device_id=dev,
            device_id_type=MESH,
        ).start()

    def await_rows(rows, sem):
        ref = x_all.at[0, 0, pl.ds(0, rows)]
        pltpu.make_async_copy(ref, ref, sem).wait()

    full = 2 * HALF

    def phase1(g):
        if g == 0:
            local.wait()
            await_rows(full - chunk_rows, a2a_recv.at[g])
        else:
            await_rows(full, a2a_recv.at[g])
        send(own, g, 0, full, recv1.at[g, 0], dev_p)
        send(own, g, 0, full, recv1.at[g, 1], dev_m)
        send(own, g, 0, full, recv1.at[g, 2], dev_y)

    def phase2(g):
        s_m, s_p = src(xm, yl), src(xp, yl)
        await_rows(full, recv1.at[g, 0])
        send(s_m, g, 0, HALF, recv2.at[g, 0], dev_p)
        await_rows(full, recv1.at[g, 1])
        send(s_p, g, HALF, full, recv2.at[g, 1], dev_m)
        send(s_m, g, CUT_LO, CUT_HI, recv2.at[g, 2], dev_y)
        send(s_p, g, CUT_LO, CUT_HI, recv2.at[g, 3], dev_y)
        await_rows(full, recv1.at[g, 2])
        send(pair, g, 0, CUT_LO, recv2.at[g, 4], dev_p)
        send(pair, g, CUT_HI, full, recv2.at[g, 5], dev_m)
        send(pair, g, CUT_HI, full, recv2.at[g, 4], dev_p)
        send(pair, g, 0, CUT_LO, recv2.at[g, 5], dev_m)

    cut = CUT_HI - CUT_LO

    def phase3(g):
        s_m, s_p = src(xm, 1 - yl), src(xp, 1 - yl)
        await_rows(HALF, recv2.at[g, 0])
        await_rows(HALF, recv2.at[g, 1])
        send(src(x2, yl), g, CUT_LO, CUT_HI, recv3.at[g, 0], dev_y)
        await_rows(full - cut, recv2.at[g, 4])
        send(s_m, g, 0, CUT_LO, recv3.at[g, 1], dev_p)
        await_rows(full - cut, recv2.at[g, 5])
        send(s_p, g, CUT_HI, full, recv3.at[g, 2], dev_m)
        await_rows(cut, recv2.at[g, 2])
        await_rows(cut, recv2.at[g, 3])

    def arrived(g):
        await_rows(cut, recv3.at[g, 0])
        await_rows(CUT_LO, recv3.at[g, 1])
        await_rows(full - CUT_HI, recv3.at[g, 2])

    half_rows = 2 * HALF
    width = x_all.shape[3]

    def block_rows(b, g0):
        other = b + 1 - 2 * (b % 2)
        same = x_all[b, g0 : g0 + 2, 0:HALF, :].reshape(half_rows, width)
        cross = x_all[other, g0 : g0 + 2, HALF:full, :].reshape(half_rows, width)
        return jnp.concatenate([same, cross], axis=0)

    def stack_step(g0, first, last):
        mine = block_rows(own, g0).astype(jnp.float32)
        parts = mine.reshape(2 * half_rows // chunk_rows, chunk_rows, width)
        h = chunk_rows // 2
        swapped = jnp.concatenate([parts[:, h:, :], -parts[:, :h, :]], axis=1)
        swapped = swapped.reshape(2 * half_rows, width)
        re_t = mine.T
        left[0:width, :] = re_t.astype(jnp.bfloat16)
        left[width:, :] = swapped.T.astype(jnp.bfloat16)
        squares = re_t * re_t
        lanes = squares[:, 0:128]
        for k in range(128, 2 * half_rows, 128):
            lanes = lanes + squares[:, k : k + 128]
        if first:
            rowpow[...] = lanes
        else:
            rowpow[...] += lanes
        mean = 1.0 / (2 * windows)
        if last:
            total = jnp.sum(rowpow[...], axis=1, keepdims=True) * mean
            row_scale = lax.rsqrt(total + EPSILON) * (1.0 / math.sqrt(windows))
            rowpow[...] = jnp.broadcast_to(row_scale, rowpow.shape)

        def body(b, carry):
            right = block_rows(b, g0)
            wide = right.astype(jnp.float32)
            sq = jnp.sum((wide * wide).reshape(2 * half_rows // 8, 8, width), axis=0)
            if not first:
                sq = sq + colpow[b]
            if not last:
                colpow[b] = sq
            else:
                col = lax.rsqrt(jnp.sum(sq, axis=0, keepdims=True) * mean + EPSILON)
            for part in (0, 1):
                product = jnp.dot(
                    left[part * width : (part + 1) * width, :], right, preferred_element_type=jnp.float32
                )
                if not first:
                    product = product + acc[b, part]
                if not last:
                    acc[b, part] = product
                else:
                    prod[b, part] = (product * rowpow[:, 0:1] * col).astype(jnp.bfloat16)
            return carry

        lax.fori_loop(0, NBLK, body, 0)

    for it in range(GROUPS + 3):
        if it < GROUPS:
            phase1(it)
        if 1 <= it < GROUPS + 1:
            phase2(it - 1)
        if 2 <= it < GROUPS + 2:
            phase3(it - 2)
        if it >= 3:
            done = it - 3
            arrived(done)
            if done % 2 == 1:
                stack_step(done - 1, done == 1, done == GROUPS - 1)

    sent = tempered.at[0:31]
    pltpu.make_async_copy(sent, sent, a2a_send).wait()
    sent = x_all.at[0:7]
    pltpu.make_async_copy(sent, sent, ag_send).wait()


def place_kernel(table, prod, out, sem):
    c = lax.axis_index("chan")
    width = prod.shape[2]
    copies = []
    for s in range(NBLK):
        copy = pltpu.make_async_copy(
            prod.at[table[c, s]], out.at[0, :, :, pl.ds(s * width, width)], sem.at[s]
        )
        copy.start()
        copies.append(copy)
    for copy in copies:
        copy.wait()


def per_device(spectra, flags, pair_table):
    local, bins, parts, width = spectra.shape
    windows = local * lax.axis_size("win")
    raw = spectra.astype(jnp.float32)
    band = jnp.mean(raw * raw, axis=(1, 2), keepdims=True)
    validity = flags.astype(jnp.float32)[:, None, None, None]
    tempered = (raw * lax.rsqrt(band + EPSILON) * validity).astype(jnp.bfloat16)
    chunk_rows = local * parts
    tempered = tempered.transpose(1, 2, 0, 3).reshape(bins, chunk_rows, width)

    vmem = pl.BlockSpec(memory_space=pltpu.VMEM)
    prod = pl.pallas_call(
        functools.partial(gather_stack_kernel, chunk_rows, windows=windows),
        out_shape=jax.ShapeDtypeStruct((NBLK, 2, width, width), jnp.bfloat16),
        in_specs=[vmem],
        out_specs=vmem,
        scratch_shapes=[
            pltpu.VMEM((NBLK, GROUPS, 2 * HALF, width), jnp.bfloat16),
            pltpu.VMEM((NBLK, 2, width, width), jnp.float32),
            pltpu.VMEM((2 * width, 4 * HALF), jnp.bfloat16),
            pltpu.VMEM((NBLK, 8, width), jnp.float32),
            pltpu.VMEM((width, 128), jnp.float32),
            pltpu.SemaphoreType.DMA,
            pltpu.SemaphoreType.DMA((GROUPS,)),
            pltpu.SemaphoreType.DMA,
            pltpu.SemaphoreType.DMA,
            pltpu.SemaphoreType.DMA((GROUPS, 3)),
            pltpu.SemaphoreType.DMA((GROUPS, 6)),
            pltpu.SemaphoreType.DMA((GROUPS, 3)),
        ],
        compiler_params=pltpu.CompilerParams(
            collective_id=0, has_side_effects=True, vmem_limit_bytes=56 * 1024 * 1024
        ),
        name="gather_stack",
    )(tempered)

    return pl.pallas_call(
        place_kernel,
        out_shape=jax.ShapeDtypeStruct((1, 2, width, NBLK * width), jnp.bfloat16),
        in_specs=[pl.BlockSpec(memory_space=pltpu.SMEM), vmem],
        out_specs=pl.BlockSpec(memory_space=pl.ANY),
        scratch_shapes=[pltpu.SemaphoreType.DMA((NBLK,))],
        name="place_blocks",
    )(pair_table, prod)


def solution(mesh):
    return jax.shard_map(
        per_device,
        mesh=mesh,
        in_specs=(P("win", None, None, "chan"), P("win"), P()),
        out_specs=P("win", None, "chan", None),
        check_vma=False,
    )
```

```python
import functools
import math

import jax
import jax.numpy as jnp
from jax import lax
from jax.experimental import pallas as pl
from jax.experimental.pallas import tpu as pltpu
from jax.sharding import PartitionSpec as P

EPSILON = 1e-05
MESH = pl.DeviceIdType.MESH

NX = 4
NZ = 8
GROUPS = 8
OFFSETS = (0, 1, -1, 2, -2, 3, -3, 4)
NBLK = 8
HALF = 96
CUT_LO = 64
CUT_HI = (144, 160, 144, 160, 144, 160, 144, 144)
STEPS = ((0, 2), (2, 2), (4, 2), (6, 2))
GATE = 3


def block_rows(x_all, b, g0, groups):
    other = b + 1 - 2 * (b % 2)
    rows, width = groups * HALF, x_all.shape[3]
    same = x_all[b, g0 : g0 + groups, 0:HALF, :].reshape(rows, width)
    cross = x_all[other, g0 : g0 + groups, HALF : 2 * HALF, :].reshape(rows, width)
    return jnp.concatenate([same, cross], axis=0)


def build_left(x_all, own, g0, groups, chunk_rows, left, rowpow, first):
    rows, width = 2 * groups * HALF, x_all.shape[3]
    mine = block_rows(x_all, own, g0, groups).astype(jnp.float32)
    parts = mine.reshape(rows // chunk_rows, chunk_rows, width)
    h = chunk_rows // 2
    swapped = jnp.concatenate([parts[:, h:, :], -parts[:, :h, :]], axis=1).reshape(rows, width)
    re_t = mine.T
    left[0:width, 0:rows] = re_t.astype(jnp.bfloat16)
    left[width:, 0:rows] = swapped.T.astype(jnp.bfloat16)
    squares = re_t * re_t
    lanes = squares[:, 0:128]
    for k in range(128, rows, 128):
        lanes = lanes + squares[:, k : k + 128]
    rowpow[...] = lanes if first else rowpow[...] + lanes


def squares_of(right):
    wide = right.astype(jnp.float32)
    return jnp.sum((wide * wide).reshape(right.shape[0] // 8, 8, right.shape[1]), axis=0)


def gather_stack_kernel(
    flags,
    spectra,
    x_all,
    acc,
    left,
    colpow,
    rowpow,
    wide,
    tempered,
    a2a_send,
    a2a_recv,
    local_sem,
    ag_send,
    recv1,
    recv2,
    recv3,
):
    local_windows = spectra.shape[0]
    bins = wide.shape[0]
    chunk_rows = tempered.shape[1]
    c = lax.axis_index("chan")
    w = lax.axis_index("win")
    x, yl = c // 2, c % 2
    yh, z, core = w // 16, (w // 2) % NZ, w % 2
    xp = (x + 1 + 2 * core) % NX
    xm = (x + 3 + 2 * core) % NX
    x2 = (x + 2) % NX

    def src(xx, yy):
        return 2 * xx + yy

    own = src(x, yl)
    pair = src(x, 1 - yl)
    dev_p = (src(xp, yl), w)
    dev_m = (src(xm, yl), w)
    dev_y = (pair, w)

    def peer(zz, other_half, other_core):
        cc = c if not other_half else pair
        hh = yh if not other_half else 1 - yh
        kk = core if not other_core else 1 - core
        return (cc, hh * 16 + zz * 2 + kk)

    barrier = pltpu.get_barrier_semaphore()
    count = 0
    for off in OFFSETS:
        zz = (z - off) % NZ
        for other_half in (0, 1):
            for other_core in (0, 1):
                if off == 0 and not other_half and not other_core:
                    continue
                pl.semaphore_signal(
                    barrier, inc=1, device_id=peer(zz, other_half, other_core), device_id_type=MESH
                )
                count += 1
    for dev in (dev_p, dev_m, dev_y):
        pl.semaphore_signal(barrier, inc=1, device_id=dev, device_id_type=MESH)
        count += 1

    odd = lax.broadcasted_iota(jnp.int32, (8, 128), 0) % 2

    def temper(i, carry):
        raw = spectra[i].astype(jnp.float32).reshape(bins, 8, 128)
        power = jnp.sum(raw * raw, axis=0)
        power = power + jnp.where(odd == 0, pltpu.roll(power, 7, 0), pltpu.roll(power, 1, 0))
        scale = lax.rsqrt(power * (1.0 / (2 * bins)) + EPSILON) * flags[i].astype(jnp.float32)
        wide[:, pl.ds(pl.multiple_of(i * 8, 8), 8), :] = raw * scale
        return carry

    lax.fori_loop(0, local_windows, temper, 0)

    def arrange(b):
        for tile in range(4):
            re = wide[b, pl.ds(2 * tile, local_windows, stride=8), :]
            im = wide[b, pl.ds(2 * tile + 1, local_windows, stride=8), :]
            both = jnp.concatenate([re, im], axis=0)
            tempered[b, :, tile * 128 : (tile + 1) * 128] = both.astype(jnp.bfloat16)

    pl.semaphore_wait(barrier, count)

    local = None
    for g, off in enumerate(OFFSETS):
        zz = (z - off) % NZ
        for other_half in (0, 1):
            for other_core in (0, 1):
                dev = peer(zz, other_half, other_core)
                arrange(dev[1])
                row = other_half * HALF + core * chunk_rows
                row = pl.multiple_of(row, 16)
                if off == 0 and not other_half and not other_core:
                    local = pltpu.make_async_copy(
                        tempered.at[w], x_all.at[own, g, pl.ds(row, chunk_rows)], local_sem
                    )
                    local.start()
                    continue
                entry = own if not other_half else pair
                pltpu.make_async_remote_copy(
                    src_ref=tempered.at[dev[1]],
                    dst_ref=x_all.at[entry, g, pl.ds(row, chunk_rows)],
                    send_sem=a2a_send,
                    recv_sem=a2a_recv.at[g],
                    device_id=dev,
                    device_id_type=MESH,
                ).start()

    def send(s, g, lo, hi, recv_sem, dev):
        ref = x_all.at[s, g, pl.ds(lo, hi - lo)]
        pltpu.make_async_remote_copy(
            src_ref=ref,
            dst_ref=ref,
            send_sem=ag_send,
            recv_sem=recv_sem,
            device_id=dev,
            device_id_type=MESH,
        ).start()

    def await_rows(rows, sem):
        ref = x_all.at[0, 0, pl.ds(0, rows)]
        pltpu.make_async_copy(ref, ref, sem).wait()

    full = 2 * HALF

    def phase1(g):
        if g == 0:
            local.wait()
            await_rows(full - chunk_rows, a2a_recv.at[g])
        else:
            await_rows(full, a2a_recv.at[g])
        send(own, g, 0, full, recv1.at[g, 0], dev_p)
        send(own, g, 0, full, recv1.at[g, 1], dev_m)
        send(own, g, 0, full, recv1.at[g, 2], dev_y)

    def phase2(g):
        s_m, s_p = src(xm, yl), src(xp, yl)
        await_rows(full, recv1.at[g, 0])
        send(s_m, g, 0, HALF, recv2.at[g, 0], dev_p)
        await_rows(full, recv1.at[g, 1])
        send(s_p, g, HALF, full, recv2.at[g, 1], dev_m)
        send(s_m, g, CUT_LO, CUT_HI[g], recv2.at[g, 2], dev_y)
        send(s_p, g, CUT_LO, CUT_HI[g], recv2.at[g, 3], dev_y)
        await_rows(full, recv1.at[g, 2])
        send(pair, g, 0, CUT_LO, recv2.at[g, 4], dev_p)
        send(pair, g, CUT_HI[g], full, recv2.at[g, 5], dev_m)
        send(pair, g, CUT_HI[g], full, recv2.at[g, 4], dev_p)
        send(pair, g, 0, CUT_LO, recv2.at[g, 5], dev_m)

    def phase3(g):
        s_m, s_p = src(xm, 1 - yl), src(xp, 1 - yl)
        cut = CUT_HI[g] - CUT_LO
        await_rows(HALF, recv2.at[g, 0])
        await_rows(HALF, recv2.at[g, 1])
        send(src(x2, yl), g, CUT_LO, CUT_HI[g], recv3.at[g, 0], dev_y)
        await_rows(full - cut, recv2.at[g, 4])
        send(s_m, g, 0, CUT_LO, recv3.at[g, 1], dev_p)
        await_rows(full - cut, recv2.at[g, 5])
        send(s_p, g, CUT_HI[g], full, recv3.at[g, 2], dev_m)
        await_rows(cut, recv2.at[g, 2])
        await_rows(cut, recv2.at[g, 3])

    def arrived(g):
        await_rows(CUT_HI[g] - CUT_LO, recv3.at[g, 0])
        await_rows(CUT_LO, recv3.at[g, 1])
        await_rows(full - CUT_HI[g], recv3.at[g, 2])

    width = x_all.shape[3]

    def stack_step(g0, groups, first):
        rows = groups * full
        build_left(x_all, own, g0, groups, chunk_rows, left, rowpow, first)

        def body(b, carry):
            right = block_rows(x_all, b, g0, groups)
            squares = squares_of(right)
            colpow[b] = squares if first else colpow[b] + squares
            for part in (0, 1):
                product = jnp.dot(
                    left[part * width : (part + 1) * width, 0:rows],
                    right,
                    preferred_element_type=jnp.float32,
                )
                acc[b, part] = product if first else acc[b, part] + product
            return carry

        lax.fori_loop(0, NBLK, body, 0)

    for it in range(GROUPS + GATE):
        if it < GROUPS:
            phase1(it)
        if 1 <= it < GROUPS + 1:
            phase2(it - 1)
        if 2 <= it < GROUPS + 2:
            phase3(it - 2)
        if it == GROUPS + 1:
            pass
        if it >= GATE:
            done = it - GATE
            arrived(done)
            for g0, groups in STEPS[:-1]:
                if done == g0 + groups - 1:
                    stack_step(g0, groups, g0 == 0)
            if done == STEPS[-1][0] - 1:
                g0, groups = STEPS[-1]
                build_left(x_all, own, g0, groups, chunk_rows, left, rowpow, False)

    sent = tempered.at[0:31]
    pltpu.make_async_copy(sent, sent, a2a_send).wait()
    sent = x_all.at[0:7]
    pltpu.make_async_copy(sent, sent, ag_send).wait()


def finish_kernel(table, x_all, acc, left, colpow, rowpow, out, buf, sem, *, windows):
    c = lax.axis_index("chan")
    width = x_all.shape[3]
    g0, groups = STEPS[-1]
    rows = 2 * groups * HALF
    mean = 1.0 / (2 * windows)
    row = lax.rsqrt(jnp.sum(rowpow[...], axis=1, keepdims=True) * mean + EPSILON)
    row = row * (1.0 / math.sqrt(windows))

    def copy(s):
        return pltpu.make_async_copy(
            buf.at[s % 2], out.at[0, :, :, pl.ds(s * width, width)], sem.at[s % 2]
        )

    for s in range(NBLK):
        b = table[c, s]
        right = block_rows(x_all, b, g0, groups)
        power = jnp.sum(colpow[b] + squares_of(right), axis=0, keepdims=True)
        col = lax.rsqrt(power * mean + EPSILON)
        if s >= 2:
            copy(s - 2).wait()
        for part in (0, 1):
            product = jnp.dot(
                left[part * width : (part + 1) * width, 0:rows],
                right,
                preferred_element_type=jnp.float32,
            )
            product = product + acc[b, part]
            buf[s % 2, part] = (product * row * col).astype(jnp.bfloat16)
        copy(s).start()
    copy(NBLK - 2).wait()
    copy(NBLK - 1).wait()


def per_device(spectra, flags, pair_table):
    local, bins, parts, width = spectra.shape
    windows = local * lax.axis_size("win")
    chunk_rows = local * parts
    tiles = width // 128
    rows = spectra.reshape(local, bins, parts, tiles, 128).transpose(0, 1, 3, 2, 4)
    rows = rows.reshape(local, bins * tiles * parts, 128)

    vmem = pl.BlockSpec(memory_space=pltpu.VMEM)
    smem = pl.BlockSpec(memory_space=pltpu.SMEM)
    left_rows = 2 * HALF * max(n for _, n in STEPS)
    kept = pl.pallas_call(
        gather_stack_kernel,
        out_shape=[
            pltpu.VMEM((NBLK, GROUPS, 2 * HALF, width), jnp.bfloat16),
            pltpu.VMEM((NBLK, 2, width, width), jnp.float32),
            pltpu.VMEM((2 * width, left_rows), jnp.bfloat16),
            pltpu.VMEM((NBLK, 8, width), jnp.float32),
            pltpu.VMEM((width, 128), jnp.float32),
        ],
        in_specs=[smem, vmem],
        out_specs=[vmem] * 5,
        scratch_shapes=[
            pltpu.VMEM((bins, local * 8, 128), jnp.float32),
            pltpu.VMEM((bins, chunk_rows, width), jnp.bfloat16),
            pltpu.SemaphoreType.DMA,
            pltpu.SemaphoreType.DMA((GROUPS,)),
            pltpu.SemaphoreType.DMA,
            pltpu.SemaphoreType.DMA,
            pltpu.SemaphoreType.DMA((GROUPS, 3)),
            pltpu.SemaphoreType.DMA((GROUPS, 6)),
            pltpu.SemaphoreType.DMA((GROUPS, 3)),
        ],
        compiler_params=pltpu.CompilerParams(
            collective_id=0, has_side_effects=True, vmem_limit_bytes=10 * 1024 * 1024
        ),
        name="gather_stack",
    )(flags, rows)

    return pl.pallas_call(
        functools.partial(finish_kernel, windows=windows),
        out_shape=jax.ShapeDtypeStruct((1, 2, width, NBLK * width), jnp.bfloat16),
        in_specs=[smem] + [vmem] * 5,
        out_specs=pl.BlockSpec(memory_space=pl.ANY),
        scratch_shapes=[
            pltpu.VMEM((2, 2, width, width), jnp.bfloat16),
            pltpu.SemaphoreType.DMA((2,)),
        ],
        compiler_params=pltpu.CompilerParams(vmem_limit_bytes=8 * 1024 * 1024),
        name="finish_blocks",
    )(pair_table, *kept)


def solution(mesh):
    return jax.shard_map(
        per_device,
        mesh=mesh,
        in_specs=(P("win", None, None, "chan"), P("win"), P()),
        out_specs=P("win", None, "chan", None),
        check_vma=False,
    )
```

```python
import functools
import math

import jax
import jax.numpy as jnp
from jax import lax
from jax.experimental import pallas as pl
from jax.experimental.pallas import tpu as pltpu
from jax.sharding import PartitionSpec as P

EPSILON = 1e-05
MESH = pl.DeviceIdType.MESH

NX = 4
NZ = 8
GROUPS = 8
OFFSETS = (0, -1, 1, -2, 2, -3, 3, 4)
NBLK = 8
HALF = 96
CUT_LO = 64
CUT_HI = (144, 160, 144, 160, 144, 160, 144, 144)
FIRST_LATE = 4
PAIR = 2
STACK_AT = (1, 3, 5, 7)
DEAL_FIRST = ((0, 0), (0, 1), (1, 0), (1, 1), (2, 0), (2, 1))
DEAL_LATER = (((3, 0), (4, 0)), ((3, 1), (4, 1)), ((5, 0), (6, 0)), ((5, 1), (6, 1)), ((7, 0),), ((7, 1),))
LOADS = 4


def block_rows(x_all, b, g0, groups):
    other = b + 1 - 2 * (b % 2)
    rows, width = groups * HALF, x_all.shape[3]
    same = x_all[b, g0 : g0 + groups, 0:HALF, :].reshape(rows, width)
    cross = x_all[other, g0 : g0 + groups, HALF : 2 * HALF, :].reshape(rows, width)
    return jnp.concatenate([same, cross], axis=0)


def build_left(x_all, own, g0, groups, chunk_rows, left, rowpow, first):
    rows, width = 2 * groups * HALF, x_all.shape[3]
    mine = block_rows(x_all, own, g0, groups).astype(jnp.float32)
    parts = mine.reshape(rows // chunk_rows, chunk_rows, width)
    h = chunk_rows // 2
    swapped = jnp.concatenate([parts[:, h:, :], -parts[:, :h, :]], axis=1).reshape(rows, width)
    re_t = mine.T
    left[0:width, 0:rows] = re_t.astype(jnp.bfloat16)
    left[width:, 0:rows] = swapped.T.astype(jnp.bfloat16)
    squares = re_t * re_t
    lanes = squares[:, 0:128]
    for k in range(128, rows, 128):
        lanes = lanes + squares[:, k : k + 128]
    rowpow[...] = lanes if first else rowpow[...] + lanes


def squares_of(right):
    wide = right.astype(jnp.float32)
    return jnp.sum((wide * wide).reshape(right.shape[0] // 8, 8, right.shape[1]), axis=0)


def gather_stack_kernel(
    flags_hbm,
    spectra_hbm,
    prod,
    x_tail,
    acc_tail,
    left,
    colpow,
    rowpow,
    x_all,
    acc,
    flags,
    spectra,
    wide,
    tempered,
    in_sem,
    ready,
    a2a_send,
    a2a_recv,
    near_recv,
    local_sem,
    ag_send,
    recv1,
    recv2,
    recv3,
):
    local_windows = spectra.shape[0]
    bins = wide.shape[0]
    batch = local_windows // LOADS
    loads = [pltpu.make_async_copy(flags_hbm, flags, in_sem.at[LOADS])]
    for i in range(LOADS):
        part = pl.ds(i * batch, batch)
        loads.append(pltpu.make_async_copy(spectra_hbm.at[part], spectra.at[part], in_sem.at[i]))
    for load in loads:
        load.start()
    chunk_rows = tempered.shape[1]
    c = lax.axis_index("chan")
    w = lax.axis_index("win")
    x, yl = c // 2, c % 2
    yh, z, core = w // 16, (w // 2) % NZ, w % 2
    xp = (x + 1 + 2 * core) % NX
    xm = (x + 3 + 2 * core) % NX
    x2 = (x + 2) % NX

    def src(xx, yy):
        return 2 * xx + yy

    own = src(x, yl)
    pair = src(x, 1 - yl)
    dev_p = (src(xp, yl), w)
    dev_m = (src(xm, yl), w)
    dev_y = (pair, w)

    def peer(zz, other_half, other_core):
        cc = c if not other_half else pair
        hh = yh if not other_half else 1 - yh
        kk = core if not other_core else 1 - core
        return (cc, hh * 16 + zz * 2 + kk)

    barrier = pltpu.get_barrier_semaphore()

    def greet(sems, zz):
        for other_half in (0, 1):
            for other_core in (0, 1):
                pl.semaphore_signal(
                    sems[other_half], inc=1, device_id=peer(zz, other_half, other_core), device_id_type=MESH
                )

    near = [peer(z, 0, 1), peer(z, 1, 0), peer(z, 1, 1), dev_p, dev_m, dev_y]
    for dev in near:
        pl.semaphore_signal(barrier, inc=1, device_id=dev, device_id_type=MESH)
    for k in range(1, NZ):
        zz = (z + k) % NZ

        @pl.when((zz > z) | (zz >= FIRST_LATE) & (z >= FIRST_LATE))
        def _():
            greet((barrier, barrier), zz)

    odd = lax.broadcasted_iota(jnp.int32, (8, 128), 0) % 2

    def temper(i, carry):
        raw = spectra[i].astype(jnp.float32).reshape(bins, 8, 128)
        power = jnp.sum(raw * raw, axis=0)
        power = power + jnp.where(odd == 0, pltpu.roll(power, 7, 0), pltpu.roll(power, 1, 0))
        scale = lax.rsqrt(power * (1.0 / (2 * bins)) + EPSILON) * flags[i].astype(jnp.float32)
        wide[:, pl.ds(pl.multiple_of(i * 8, 8), 8), :] = raw * scale
        return carry

    loads[0].wait()
    for i in range(LOADS):
        loads[i + 1].wait()
        lax.fori_loop(i * batch, (i + 1) * batch, temper, 0)
        if i == LOADS // 2 - 1:
            pl.semaphore_wait(barrier, len(near) + 4 * jnp.where(z < FIRST_LATE, z, NZ - 1))
            for k in range(1, NZ):

                zz = (z - k) % NZ

                @pl.when((zz < z) & (zz < FIRST_LATE))
                def _():
                    greet((ready.at[0, z], ready.at[1, z]), zz)

    def arrange(b):
        for tile in range(4):
            re = wide[b, pl.ds(2 * tile, local_windows, stride=8), :]
            im = wide[b, pl.ds(2 * tile + 1, local_windows, stride=8), :]
            both = jnp.concatenate([re, im], axis=0)
            tempered[b, :, tile * 128 : (tile + 1) * 128] = both.astype(jnp.bfloat16)

    local_row = pl.multiple_of(core * chunk_rows, 16)
    local = pltpu.make_async_copy(
        tempered.at[w], x_all.at[own, 0, pl.ds(local_row, chunk_rows)], local_sem
    )

    def deal(g, other_half):
        zz = (z - OFFSETS[g]) % NZ

        @pl.when((zz > z) & (z < FIRST_LATE))
        def _():
            pl.semaphore_wait(ready.at[other_half, zz], 2)

        for other_core in (0, 1):
            dev = peer(zz, other_half, other_core)
            arrange(dev[1])
            if g == 0 and not other_half and not other_core:
                local.start()
                continue
            row = pl.multiple_of(other_half * HALF + core * chunk_rows, 16)
            pltpu.make_async_remote_copy(
                src_ref=tempered.at[dev[1]],
                dst_ref=x_all.at[own if not other_half else pair, g, pl.ds(row, chunk_rows)],
                send_sem=a2a_send,
                recv_sem=a2a_recv.at[g] if g or other_half else near_recv,
                device_id=dev,
                device_id_type=MESH,
            ).start()

    def send(s, g, lo, hi, recv_sem, dev):
        ref = x_all.at[s, g, pl.ds(lo, hi - lo)]
        pltpu.make_async_remote_copy(
            src_ref=ref,
            dst_ref=ref,
            send_sem=ag_send,
            recv_sem=recv_sem,
            device_id=dev,
            device_id_type=MESH,
        ).start()

    def await_rows(rows, sem):
        ref = x_all.at[0, 0, pl.ds(0, rows)]
        pltpu.make_async_copy(ref, ref, sem).wait()

    full = 2 * HALF

    def phase1(g):
        cuts = [0, full]
        if g == 0:
            local.wait()
            await_rows(HALF - chunk_rows, near_recv)
            cuts = [0, HALF, full]
        for lo, hi in zip(cuts, cuts[1:]):
            if hi == full:
                await_rows(HALF if g == 0 else full, a2a_recv.at[g])
            send(own, g, lo, hi, recv1.at[g, 0], dev_p)
            send(own, g, lo, hi, recv1.at[g, 1], dev_m)
            send(own, g, lo, hi, recv1.at[g, 2], dev_y)

    def phase2(g):
        s_m, s_p = src(xm, yl), src(xp, yl)
        await_rows(full, recv1.at[g, 0])
        send(s_m, g, 0, HALF, recv2.at[g, 0], dev_p)
        await_rows(full, recv1.at[g, 1])
        send(s_p, g, HALF, full, recv2.at[g, 1], dev_m)
        send(s_m, g, CUT_LO, CUT_HI[g], recv2.at[g, 2], dev_y)
        send(s_p, g, CUT_LO, CUT_HI[g], recv2.at[g, 3], dev_y)
        await_rows(full, recv1.at[g, 2])
        send(pair, g, 0, CUT_LO, recv2.at[g, 4], dev_p)
        send(pair, g, CUT_HI[g], full, recv2.at[g, 5], dev_m)
        send(pair, g, CUT_HI[g], full, recv2.at[g, 6], dev_p)
        send(pair, g, 0, CUT_LO, recv2.at[g, 7], dev_m)

    def phase3(g):
        s_m, s_p = src(xm, 1 - yl), src(xp, 1 - yl)
        cut = CUT_HI[g] - CUT_LO
        await_rows(HALF, recv2.at[g, 0])
        await_rows(HALF, recv2.at[g, 1])
        send(src(x2, yl), g, CUT_LO, CUT_HI[g], recv3.at[g, 0], dev_y)
        await_rows(CUT_LO, recv2.at[g, 4])
        send(s_m, g, 0, CUT_LO, recv3.at[g, 1], dev_p)
        await_rows(full - CUT_HI[g], recv2.at[g, 5])
        send(s_p, g, CUT_HI[g], full, recv3.at[g, 2], dev_m)
        await_rows(cut, recv2.at[g, 2])
        await_rows(cut, recv2.at[g, 3])
        await_rows(full - CUT_HI[g], recv2.at[g, 6])
        await_rows(CUT_LO, recv2.at[g, 7])

    def arrived(g):
        await_rows(CUT_HI[g] - CUT_LO, recv3.at[g, 0])
        await_rows(CUT_LO, recv3.at[g, 1])
        await_rows(full - CUT_HI[g], recv3.at[g, 2])

    width = x_all.shape[3]
    mean = 1.0 / (2 * bins * local_windows)
    rows = PAIR * full

    def b_of(i, column):
        return src((column + 2 * (i // 2)) % NX, i % 2)

    def stack(column, count, g0):
        first, last = g0 == 0, g0 == GROUPS - PAIR
        far = column is x2
        sums = acc_tail if far else acc

        def body(i, carry):
            k = i if far else b_of(i, column)
            b = b_of(i, column)
            right = block_rows(x_all, b, g0, PAIR)
            power = squares_of(right)
            if not first:
                power = power + colpow[b]
            if last:
                col = lax.rsqrt(jnp.sum(power, axis=0, keepdims=True) * mean + EPSILON)
            else:
                colpow[b] = power

            def half(part, inner):
                product = jnp.dot(
                    left[pl.ds(pl.multiple_of(part * width, width), width), :],
                    block_rows(x_all, b, g0, PAIR),
                    preferred_element_type=jnp.float32,
                )
                if not first:
                    product = product + sums[k, part]
                if last:
                    prod[b, part] = (product * rowpow[:, 0:1] * col).astype(jnp.bfloat16)
                else:
                    sums[k, part] = product
                return inner

            lax.fori_loop(0, 2, half, 0)
            return carry

        lax.fori_loop(0, 2 * count, body, 0)

    for g, half in DEAL_FIRST:
        deal(g, half)
    for it in range(GROUPS + 3):
        if it < GROUPS:
            phase1(it)
        for g, half in DEAL_LATER[it] if it < len(DEAL_LATER) else ():
            deal(g, half)
        if 1 <= it < GROUPS + 1:
            phase2(it - 1)
        if 2 <= it < GROUPS + 2:
            phase3(it - 2)
        if it >= 3:
            arrived(it - 3)
            if it - 3 in STACK_AT and it < GROUPS + 2:
                stack(x2, 1, it - 3 - PAIR + 1)
        if it - 1 in STACK_AT:
            g0 = it - PAIR
            build_left(x_all, own, g0, PAIR, chunk_rows, left, rowpow, g0 == 0)
            if g0 == GROUPS - PAIR:
                row = lax.rsqrt(jnp.sum(rowpow[...], axis=1, keepdims=True) * mean + EPSILON)
                row = row * (1.0 / math.sqrt(bins * local_windows))
                rowpow[...] = jnp.broadcast_to(row, rowpow.shape)
            stack(x, 1, g0)
        if it - 2 in STACK_AT:
            stack((x + 1) % NX, 2, it - 2 - PAIR + 1)

    tails = [
        pltpu.make_async_copy(
            x_all.at[src(x2, i), pl.ds(GROUPS - PAIR, PAIR)], x_tail.at[i], in_sem.at[i]
        )
        for i in (0, 1)
    ]
    for tail in tails:
        tail.start()
    for tail in tails:
        tail.wait()
    sent = tempered.at[0:31]
    pltpu.make_async_copy(sent, sent, a2a_send).wait()
    sent = x_all.at[0:7]
    pltpu.make_async_copy(sent, sent, ag_send).wait()


def finish_kernel(
    table_hbm, prod_in, x_tail, acc_tail, left, colpow, rowpow, out, table, buf, sem, table_sem, *, windows
):
    c = lax.axis_index("chan")
    load = pltpu.make_async_copy(table_hbm, table, table_sem)
    load.start()
    width = x_tail.shape[3]
    mean = 1.0 / (2 * windows)
    column = (c // 2 + 2) % NX

    def copy(s, ref):
        return pltpu.make_async_copy(ref, out.at[0, :, :, pl.ds(s * width, width)], sem.at[s])

    def complete(i, carry):
        b = 2 * column + i
        right = block_rows(x_tail, i, 0, PAIR)
        power = jnp.sum(colpow[b] + squares_of(right), axis=0, keepdims=True)
        col = lax.rsqrt(power * mean + EPSILON)
        for part in (0, 1):
            product = jnp.dot(
                left[part * width : (part + 1) * width, :], right, preferred_element_type=jnp.float32
            )
            product = product + acc_tail[i, part]
            buf[i, part] = (product * rowpow[:, 0:1] * col).astype(jnp.bfloat16)
        return carry

    load.wait()
    for s in range(NBLK):
        b = table[c, s]

        @pl.when(b // 2 != column)
        def _():
            copy(s, prod_in.at[b]).start()

    lax.fori_loop(0, 2, complete, 0)
    for s in range(NBLK):
        b = table[c, s]

        @pl.when(b // 2 == column)
        def _():
            copy(s, buf.at[b % 2]).start()

    for s in range(NBLK):
        copy(s, buf.at[0]).wait()


def at_home(array):
    return pltpu.with_memory_space_constraint(array, pltpu.HBM)


def per_device(spectra, flags, pair_table):
    local, bins, parts, width = spectra.shape
    windows = local * lax.axis_size("win")
    chunk_rows = local * parts
    tiles = width // 128
    rows = spectra.reshape(local, bins, parts, tiles, 128).transpose(0, 1, 3, 2, 4)
    rows = rows.reshape(local, bins * tiles * parts, 128)

    vmem = pl.BlockSpec(memory_space=pltpu.VMEM)
    hbm = pl.BlockSpec(memory_space=pltpu.HBM)
    kept = pl.pallas_call(
        gather_stack_kernel,
        out_shape=[
            pltpu.VMEM((NBLK, 2, width, width), jnp.bfloat16),
            pltpu.VMEM((2, PAIR, 2 * HALF, width), jnp.bfloat16),
            pltpu.VMEM((2, 2, width, width), jnp.float32),
            pltpu.VMEM((2 * width, PAIR * 2 * HALF), jnp.bfloat16),
            pltpu.VMEM((NBLK, 8, width), jnp.float32),
            pltpu.VMEM((width, 128), jnp.float32),
        ],
        in_specs=[hbm, hbm],
        out_specs=[vmem] * 6,
        scratch_shapes=[
            pltpu.VMEM((NBLK, GROUPS, 2 * HALF, width), jnp.bfloat16),
            pltpu.VMEM((NBLK, 2, width, width), jnp.float32),
            pltpu.SMEM((local,), jnp.int32),
            pltpu.VMEM(rows.shape, jnp.bfloat16),
            pltpu.VMEM((bins, local * 8, 128), jnp.float32),
            pltpu.VMEM((bins, chunk_rows, width), jnp.bfloat16),
            pltpu.SemaphoreType.DMA((LOADS + 1,)),
            pltpu.SemaphoreType.REGULAR((2, NZ)),
            pltpu.SemaphoreType.DMA,
            pltpu.SemaphoreType.DMA((GROUPS,)),
            pltpu.SemaphoreType.DMA,
            pltpu.SemaphoreType.DMA,
            pltpu.SemaphoreType.DMA,
            pltpu.SemaphoreType.DMA((GROUPS, 3)),
            pltpu.SemaphoreType.DMA((GROUPS, 8)),
            pltpu.SemaphoreType.DMA((GROUPS, 3)),
        ],
        compiler_params=pltpu.CompilerParams(
            collective_id=0, has_side_effects=True, vmem_limit_bytes=40 * 1024 * 1024
        ),
        name="gather_stack",
    )(at_home(flags), at_home(rows))

    return pl.pallas_call(
        functools.partial(finish_kernel, windows=windows),
        out_shape=jax.ShapeDtypeStruct((1, 2, width, NBLK * width), jnp.bfloat16),
        in_specs=[hbm] + [vmem] * 6,
        out_specs=pl.BlockSpec(memory_space=pltpu.HBM),
        scratch_shapes=[
            pltpu.SMEM(pair_table.shape, jnp.int32),
            pltpu.VMEM((2, 2, width, width), jnp.bfloat16),
            pltpu.SemaphoreType.DMA((NBLK,)),
            pltpu.SemaphoreType.DMA,
        ],
        compiler_params=pltpu.CompilerParams(vmem_limit_bytes=8 * 1024 * 1024),
        name="finish_blocks",
    )(at_home(pair_table), *kept)


def solution(mesh):
    return jax.shard_map(
        per_device,
        mesh=mesh,
        in_specs=(P("win", None, None, "chan"), P("win"), P()),
        out_specs=P("win", None, "chan", None),
        check_vma=False,
    )
```

```python
import functools
import math

import jax
import jax.numpy as jnp
from jax import lax
from jax.experimental import pallas as pl
from jax.experimental.pallas import tpu as pltpu
from jax.sharding import PartitionSpec as P

EPSILON = 1e-05
MESH = pl.DeviceIdType.MESH

NX = 4
NZ = 8
GROUPS = 8
OFFSETS = (0, -1, 1, -2, 2, -3, 3, 4)
NBLK = 8
HALF = 96
CUT_LO = 64
CUT_HI = (144, 160, 144, 160, 144, 160, 144, 144)
FIRST_LATE = 4
PAIR = 2
STACK_AT = (1, 3, 5, 7)
DEAL_FIRST = ((0, 0), (0, 1), (1, 0), (1, 1), (2, 0), (2, 1))
DEAL_LATER = (((3, 0), (4, 0)), ((3, 1), (4, 1)), ((5, 0), (6, 0)), ((5, 1), (6, 1)), ((7, 0),), ((7, 1),))
LOADS = 4


def block_rows(x_all, b, g0, groups):
    other = b + 1 - 2 * (b % 2)
    rows, width = groups * HALF, x_all.shape[3]
    same = x_all[b, g0 : g0 + groups, 0:HALF, :].reshape(rows, width)
    cross = x_all[other, g0 : g0 + groups, HALF : 2 * HALF, :].reshape(rows, width)
    return jnp.concatenate([same, cross], axis=0)


def build_left(x_all, own, g0, groups, chunk_rows, left, rowpow, first):
    rows, width = 2 * groups * HALF, x_all.shape[3]
    mine = block_rows(x_all, own, g0, groups).astype(jnp.float32)
    parts = mine.reshape(rows // chunk_rows, chunk_rows, width)
    h = chunk_rows // 2
    swapped = jnp.concatenate([parts[:, h:, :], -parts[:, :h, :]], axis=1).reshape(rows, width)
    re_t = mine.T
    left[0:width, 0:rows] = re_t.astype(jnp.bfloat16)
    left[width:, 0:rows] = swapped.T.astype(jnp.bfloat16)
    squares = re_t * re_t
    lanes = squares[:, 0:128]
    for k in range(128, rows, 128):
        lanes = lanes + squares[:, k : k + 128]
    rowpow[...] = lanes if first else rowpow[...] + lanes


def squares_of(right):
    wide = right.astype(jnp.float32)
    return jnp.sum((wide * wide).reshape(right.shape[0] // 8, 8, right.shape[1]), axis=0)


def gather_stack_kernel(
    flags_hbm,
    spectra_hbm,
    prod,
    x_tail,
    acc_tail,
    left,
    colpow,
    rowpow,
    x_all,
    acc,
    flags,
    spectra,
    wide,
    tempered,
    in_sem,
    ready,
    a2a_send,
    a2a_recv,
    near_recv,
    local_sem,
    ag_send,
    recv1,
    recv2,
    recv3,
):
    local_windows = spectra.shape[0]
    bins = wide.shape[0]
    batch = local_windows // LOADS
    loads = [pltpu.make_async_copy(flags_hbm, flags, in_sem.at[LOADS])]
    for i in range(LOADS):
        part = pl.ds(i * batch, batch)
        loads.append(pltpu.make_async_copy(spectra_hbm.at[part], spectra.at[part], in_sem.at[i]))
    for load in loads:
        load.start()
    chunk_rows = tempered.shape[1]
    c = lax.axis_index("chan")
    w = lax.axis_index("win")
    x, yl = c // 2, c % 2
    yh, z, core = w // 16, (w // 2) % NZ, w % 2
    xp = (x + 1 + 2 * core) % NX
    xm = (x + 3 + 2 * core) % NX
    x2 = (x + 2) % NX

    def src(xx, yy):
        return 2 * xx + yy

    own = src(x, yl)
    pair = src(x, 1 - yl)
    dev_p = (src(xp, yl), w)
    dev_m = (src(xm, yl), w)
    dev_y = (pair, w)

    def peer(zz, other_half, other_core):
        cc = c if not other_half else pair
        hh = yh if not other_half else 1 - yh
        kk = core if not other_core else 1 - core
        return (cc, hh * 16 + zz * 2 + kk)

    barrier = pltpu.get_barrier_semaphore()

    def greet(sems, zz):
        for other_half in (0, 1):
            for other_core in (0, 1):
                pl.semaphore_signal(
                    sems[other_half], inc=1, device_id=peer(zz, other_half, other_core), device_id_type=MESH
                )

    near = [peer(z, 0, 1), peer(z, 1, 0), peer(z, 1, 1), dev_p, dev_m, dev_y]
    for dev in near:
        pl.semaphore_signal(barrier, inc=1, device_id=dev, device_id_type=MESH)
    for k in range(1, NZ):
        zz = (z + k) % NZ

        @pl.when((zz > z) | (zz >= FIRST_LATE) & (z >= FIRST_LATE))
        def _():
            greet((barrier, barrier), zz)

    odd = lax.broadcasted_iota(jnp.int32, (8, 128), 0) % 2

    def temper(i, carry):
        raw = spectra[i].astype(jnp.float32).reshape(bins, 8, 128)
        power = jnp.sum(raw * raw, axis=0)
        power = power + jnp.where(odd == 0, pltpu.roll(power, 7, 0), pltpu.roll(power, 1, 0))
        scale = lax.rsqrt(power * (1.0 / (2 * bins)) + EPSILON) * flags[i].astype(jnp.float32)
        wide[:, pl.ds(pl.multiple_of(i * 8, 8), 8), :] = raw * scale
        return carry

    loads[0].wait()
    for i in range(LOADS):
        loads[i + 1].wait()
        lax.fori_loop(i * batch, (i + 1) * batch, temper, 0)
        if i == LOADS // 2 - 1:
            pl.semaphore_wait(barrier, len(near) + 4 * jnp.where(z < FIRST_LATE, z, NZ - 1))
            for k in range(1, NZ):

                zz = (z - k) % NZ

                @pl.when((zz < z) & (zz < FIRST_LATE))
                def _():
                    greet((ready.at[0, z], ready.at[1, z]), zz)

    def arrange(b):
        for tile in range(4):
            re = wide[b, pl.ds(2 * tile, local_windows, stride=8), :]
            im = wide[b, pl.ds(2 * tile + 1, local_windows, stride=8), :]
            both = jnp.concatenate([re, im], axis=0)
            tempered[b, :, tile * 128 : (tile + 1) * 128] = both.astype(jnp.bfloat16)

    local_row = pl.multiple_of(core * chunk_rows, 16)
    local = pltpu.make_async_copy(
        tempered.at[w], x_all.at[own, 0, pl.ds(local_row, chunk_rows)], local_sem
    )

    def deal(g, other_half):
        zz = (z - OFFSETS[g]) % NZ
        slot = jnp.where(zz == 0, 3 - g, g) if g in (1, 2) else g

        @pl.when((zz > z) & (z < FIRST_LATE))
        def _():
            pl.semaphore_wait(ready.at[other_half, zz], 2)

        for other_core in (0, 1):
            dev = peer(zz, other_half, other_core)
            arrange(dev[1])
            if g == 0 and not other_half and not other_core:
                local.start()
                continue
            row = pl.multiple_of(other_half * HALF + core * chunk_rows, 16)
            pltpu.make_async_remote_copy(
                src_ref=tempered.at[dev[1]],
                dst_ref=x_all.at[own if not other_half else pair, slot, pl.ds(row, chunk_rows)],
                send_sem=a2a_send,
                recv_sem=a2a_recv.at[slot] if g or other_half else near_recv,
                device_id=dev,
                device_id_type=MESH,
            ).start()

    def send(s, g, lo, hi, recv_sem, dev):
        ref = x_all.at[s, g, pl.ds(lo, hi - lo)]
        pltpu.make_async_remote_copy(
            src_ref=ref,
            dst_ref=ref,
            send_sem=ag_send,
            recv_sem=recv_sem,
            device_id=dev,
            device_id_type=MESH,
        ).start()

    def await_rows(rows, sem):
        ref = x_all.at[0, 0, pl.ds(0, rows)]
        pltpu.make_async_copy(ref, ref, sem).wait()

    full = 2 * HALF

    def phase1(g):
        cuts = [0, full]
        if g == 0:
            local.wait()
            await_rows(HALF - chunk_rows, near_recv)
            cuts = [0, HALF, full]
        for lo, hi in zip(cuts, cuts[1:]):
            if hi == full:
                await_rows(HALF if g == 0 else full, a2a_recv.at[g])
            send(own, g, lo, hi, recv1.at[g, 0], dev_p)
            send(own, g, lo, hi, recv1.at[g, 1], dev_m)
            send(own, g, lo, hi, recv1.at[g, 2], dev_y)

    def phase2(g):
        s_m, s_p = src(xm, yl), src(xp, yl)
        await_rows(full, recv1.at[g, 0])
        send(s_m, g, 0, HALF, recv2.at[g, 0], dev_p)
        await_rows(full, recv1.at[g, 1])
        send(s_p, g, HALF, full, recv2.at[g, 1], dev_m)
        send(s_m, g, CUT_LO, CUT_HI[g], recv2.at[g, 2], dev_y)
        send(s_p, g, CUT_LO, CUT_HI[g], recv2.at[g, 3], dev_y)
        await_rows(full, recv1.at[g, 2])
        send(pair, g, 0, CUT_LO, recv2.at[g, 4], dev_p)
        send(pair, g, CUT_HI[g], full, recv2.at[g, 5], dev_m)
        send(pair, g, CUT_HI[g], full, recv2.at[g, 6], dev_p)
        send(pair, g, 0, CUT_LO, recv2.at[g, 7], dev_m)

    def phase3(g):
        s_m, s_p = src(xm, 1 - yl), src(xp, 1 - yl)
        cut = CUT_HI[g] - CUT_LO
        await_rows(HALF, recv2.at[g, 0])
        await_rows(HALF, recv2.at[g, 1])
        send(src(x2, yl), g, CUT_LO, CUT_HI[g], recv3.at[g, 0], dev_y)
        await_rows(CUT_LO, recv2.at[g, 4])
        send(s_m, g, 0, CUT_LO, recv3.at[g, 1], dev_p)
        await_rows(full - CUT_HI[g], recv2.at[g, 5])
        send(s_p, g, CUT_HI[g], full, recv3.at[g, 2], dev_m)
        await_rows(cut, recv2.at[g, 2])
        await_rows(cut, recv2.at[g, 3])
        await_rows(full - CUT_HI[g], recv2.at[g, 6])
        await_rows(CUT_LO, recv2.at[g, 7])

    def arrived(g):
        await_rows(CUT_HI[g] - CUT_LO, recv3.at[g, 0])
        await_rows(CUT_LO, recv3.at[g, 1])
        await_rows(full - CUT_HI[g], recv3.at[g, 2])

    width = x_all.shape[3]
    mean = 1.0 / (2 * bins * local_windows)
    rows = PAIR * full

    def b_of(i, column):
        return src((column + 2 * (i // 2)) % NX, i % 2)

    def stack(column, count, g0):
        first, last = g0 == 0, g0 == GROUPS - PAIR
        far = column is x2
        sums = acc_tail if far else acc

        def body(i, carry):
            k = i if far else b_of(i, column)
            b = b_of(i, column)
            right = block_rows(x_all, b, g0, PAIR)
            power = squares_of(right)
            if not first:
                power = power + colpow[b]
            if last:
                col = lax.rsqrt(jnp.sum(power, axis=0, keepdims=True) * mean + EPSILON)
            else:
                colpow[b] = power

            def half(part, inner):
                product = jnp.dot(
                    left[pl.ds(pl.multiple_of(part * width, width), width), :],
                    block_rows(x_all, b, g0, PAIR),
                    preferred_element_type=jnp.float32,
                )
                if not first:
                    product = product + sums[k, part]
                if last:
                    prod[b, part] = (product * rowpow[:, 0:1] * col).astype(jnp.bfloat16)
                else:
                    sums[k, part] = product
                return inner

            lax.fori_loop(0, 2, half, 0)
            return carry

        lax.fori_loop(0, 2 * count, body, 0)

    for g, half in DEAL_FIRST:
        deal(g, half)
    for it in range(GROUPS + 3):
        if it < GROUPS:
            phase1(it)
        for g, half in DEAL_LATER[it] if it < len(DEAL_LATER) else ():
            deal(g, half)
        if 1 <= it < GROUPS + 1:
            phase2(it - 1)
        if 2 <= it < GROUPS + 2:
            phase3(it - 2)
        if it >= 3:
            arrived(it - 3)
            if it - 3 in STACK_AT and it < GROUPS + 2:
                stack(x2, 1, it - 3 - PAIR + 1)
        if it - 1 in STACK_AT:
            g0 = it - PAIR
            build_left(x_all, own, g0, PAIR, chunk_rows, left, rowpow, g0 == 0)
            if g0 == GROUPS - PAIR:
                row = lax.rsqrt(jnp.sum(rowpow[...], axis=1, keepdims=True) * mean + EPSILON)
                row = row * (1.0 / math.sqrt(bins * local_windows))
                rowpow[...] = jnp.broadcast_to(row, rowpow.shape)
            stack(x, 1, g0)
        if it - 2 in STACK_AT:
            stack((x + 1) % NX, 2, it - 2 - PAIR + 1)

    tails = [
        pltpu.make_async_copy(
            x_all.at[src(x2, i), pl.ds(GROUPS - PAIR, PAIR)], x_tail.at[i], in_sem.at[i]
        )
        for i in (0, 1)
    ]
    for tail in tails:
        tail.start()
    for tail in tails:
        tail.wait()
    sent = tempered.at[0:31]
    pltpu.make_async_copy(sent, sent, a2a_send).wait()
    sent = x_all.at[0:7]
    pltpu.make_async_copy(sent, sent, ag_send).wait()


def finish_kernel(
    table_hbm, prod_in, x_tail, acc_tail, left, colpow, rowpow, out, table, buf, sem, table_sem, *, windows
):
    c = lax.axis_index("chan")
    load = pltpu.make_async_copy(table_hbm, table, table_sem)
    load.start()
    width = x_tail.shape[3]
    mean = 1.0 / (2 * windows)
    column = (c // 2 + 2) % NX

    def copy(s, ref):
        return pltpu.make_async_copy(ref, out.at[0, :, :, pl.ds(s * width, width)], sem.at[s])

    def complete(i, carry):
        b = 2 * column + i
        right = block_rows(x_tail, i, 0, PAIR)
        power = jnp.sum(colpow[b] + squares_of(right), axis=0, keepdims=True)
        col = lax.rsqrt(power * mean + EPSILON)
        for part in (0, 1):
            product = jnp.dot(
                left[part * width : (part + 1) * width, :], right, preferred_element_type=jnp.float32
            )
            product = product + acc_tail[i, part]
            buf[i, part] = (product * rowpow[:, 0:1] * col).astype(jnp.bfloat16)
        return carry

    load.wait()
    for s in range(NBLK):
        b = table[c, s]

        @pl.when(b // 2 != column)
        def _():
            copy(s, prod_in.at[b]).start()

    lax.fori_loop(0, 2, complete, 0)
    for s in range(NBLK):
        b = table[c, s]

        @pl.when(b // 2 == column)
        def _():
            copy(s, buf.at[b % 2]).start()

    for s in range(NBLK):
        copy(s, buf.at[0]).wait()


def at_home(array):
    return pltpu.with_memory_space_constraint(array, pltpu.HBM)


def per_device(spectra, flags, pair_table):
    local, bins, parts, width = spectra.shape
    windows = local * lax.axis_size("win")
    chunk_rows = local * parts
    tiles = width // 128
    rows = spectra.reshape(local, bins, parts, tiles, 128).transpose(0, 1, 3, 2, 4)
    rows = rows.reshape(local, bins * tiles * parts, 128)

    vmem = pl.BlockSpec(memory_space=pltpu.VMEM)
    hbm = pl.BlockSpec(memory_space=pltpu.HBM)
    kept = pl.pallas_call(
        gather_stack_kernel,
        out_shape=[
            pltpu.VMEM((NBLK, 2, width, width), jnp.bfloat16),
            pltpu.VMEM((2, PAIR, 2 * HALF, width), jnp.bfloat16),
            pltpu.VMEM((2, 2, width, width), jnp.float32),
            pltpu.VMEM((2 * width, PAIR * 2 * HALF), jnp.bfloat16),
            pltpu.VMEM((NBLK, 8, width), jnp.float32),
            pltpu.VMEM((width, 128), jnp.float32),
        ],
        in_specs=[hbm, hbm],
        out_specs=[vmem] * 6,
        scratch_shapes=[
            pltpu.VMEM((NBLK, GROUPS, 2 * HALF, width), jnp.bfloat16),
            pltpu.VMEM((NBLK, 2, width, width), jnp.float32),
            pltpu.SMEM((local,), jnp.int32),
            pltpu.VMEM(rows.shape, jnp.bfloat16),
            pltpu.VMEM((bins, local * 8, 128), jnp.float32),
            pltpu.VMEM((bins, chunk_rows, width), jnp.bfloat16),
            pltpu.SemaphoreType.DMA((LOADS + 1,)),
            pltpu.SemaphoreType.REGULAR((2, NZ)),
            pltpu.SemaphoreType.DMA,
            pltpu.SemaphoreType.DMA((GROUPS,)),
            pltpu.SemaphoreType.DMA,
            pltpu.SemaphoreType.DMA,
            pltpu.SemaphoreType.DMA,
            pltpu.SemaphoreType.DMA((GROUPS, 3)),
            pltpu.SemaphoreType.DMA((GROUPS, 8)),
            pltpu.SemaphoreType.DMA((GROUPS, 3)),
        ],
        compiler_params=pltpu.CompilerParams(
            collective_id=0, has_side_effects=True, vmem_limit_bytes=40 * 1024 * 1024
        ),
        name="gather_stack",
    )(at_home(flags), at_home(rows))

    return pl.pallas_call(
        functools.partial(finish_kernel, windows=windows),
        out_shape=jax.ShapeDtypeStruct((1, 2, width, NBLK * width), jnp.bfloat16),
        in_specs=[hbm] + [vmem] * 6,
        out_specs=pl.BlockSpec(memory_space=pltpu.HBM),
        scratch_shapes=[
            pltpu.SMEM(pair_table.shape, jnp.int32),
            pltpu.VMEM((2, 2, width, width), jnp.bfloat16),
            pltpu.SemaphoreType.DMA((NBLK,)),
            pltpu.SemaphoreType.DMA,
        ],
        compiler_params=pltpu.CompilerParams(vmem_limit_bytes=8 * 1024 * 1024),
        name="finish_blocks",
    )(at_home(pair_table), *kept)


def solution(mesh):
    return jax.shard_map(
        per_device,
        mesh=mesh,
        in_specs=(P("win", None, None, "chan"), P("win"), P()),
        out_specs=P("win", None, "chan", None),
        check_vma=False,
    )
```
